32 devices in a mesh: depth: 2 (over core), rows: 2 (over x), shots: 8 (over z, y).
Axes of the slice: x: 2, y: 2, z: 4, core: 2. Of those that a mesh axis runs over, the one named last changes fastest.
Arguments:
- sources: float32 [2, 2, 1024, 1024], P('depth', None, 'rows', 'shots'), may hold values from -6 to 6
- factor: float32 [2, 2, 1024, 1024], P('depth', None, ('rows', 'shots')), may hold values from -0.09375 to 0.09375
- block_mask: int32 [2, 2, 8, 8], P('depth'), may hold values 0 or 1
- inverse_diagonal: float32 [2, 2, 1024, 1024], P('depth', None, None, 'rows'), may hold values from -1.2 to 1.2, as said below
Outputs:
- solution: float32 [2, 2, 1024, 1024], P('depth', None, 'rows', 'shots')
The draws below stay inside these ranges and needn't reach their ends.
Inputs may be any that keep to these rules, and one draw needn't show every extreme that they name: Each block inverse_diagonal[d, m] is lower triangular with diagonal entries between 0.8 and 1.2.
All inputs are finite; a program needn't handle non-finite values. No bound on the sum of `block_mask` on one device may be relied on, other than what follows from the above.
Results may differ from the reference program's by a relative error of at most 0.0001.
Values sent between devices are 32-bit elements; how exact they have to be, the bound alone decides.
No kernel may reach another device: no remote copies, remote signals or barrier semaphores. Data moves between devices by JAX's collectives and lax.ppermute only.
A program may use at most 64 MiB of HBM per device.

```python
import jax
import jax.numpy as jnp
from jax import lax

SUPER = 1024
BLOCK = 128
NRHS = 1024
LEVELS = 2
PAIRS = 2
N_DEPTH = 2


def draw_inverse_diagonal(key, part):
    shape = (N_DEPTH, LEVELS, SUPER, SUPER)
    first_key = jax.random.fold_in(key, 11)
    second_key = jax.random.fold_in(key, 23)
    noise = jax.random.normal(first_key, shape, jnp.float32)
    diagonal_values = jax.random.uniform(second_key, (N_DEPTH, LEVELS, SUPER, 1), jnp.float32, 0.8, 1.2)
    identity = jnp.eye(SUPER, dtype=jnp.float32)
    strict = jnp.tril(noise, -1) * (0.7 / SUPER ** 0.5)
    return strict + identity * diagonal_values


def place_ends(values, rng, smallest, high):
    longest = values.shape.index(max(values.shape))
    spots = []
    for shift in (0, 1):
        where = [jax.random.randint(jax.random.fold_in(rng, axis), (), 0, length) for axis, length in enumerate(values.shape)]
        where[longest] = (where[longest] + shift) % values.shape[longest]
        spots.append(tuple(where))
    return values.at[spots[0]].set(smallest).at[spots[1]].set(high)


def block_scale(stream_key, dims, pieces, low, largest):
    level, own = 1.0, jax.random.fold_in(stream_key, 6)
    for dim, blocks in pieces:
        steps = jnp.exp(jax.random.uniform(jax.random.fold_in(own, dim), (blocks,), jnp.float32, low / len(pieces), largest / len(pieces)))
        level = level * jnp.repeat(steps, dims[dim] // blocks).reshape([-1 if axis == dim else 1 for axis in range(len(dims))])
    return level


def normal_values(own_key, dims, deviation, most, pieces=(), kind=jnp.bfloat16):
    result = deviation * jax.random.normal(own_key, dims, jnp.float32)
    if pieces:
        result = result * block_scale(own_key, dims, pieces, -0.22, 0.18)
    return jnp.clip(result, -most, most).astype(kind)


def setup_inputs(seed: int = 0) -> dict:
    key_list = jax.random.split(jax.random.key(seed), 5)
    return {
        "sources": normal_values(key_list[0], (N_DEPTH, LEVELS, SUPER, NRHS), 1.0, 6.0, ((0, 2), (2, 2), (3, 8)), jnp.float32),
        "factor": normal_values(key_list[1], (N_DEPTH, PAIRS, SUPER, SUPER), (2 * SUPER * N_DEPTH) ** -0.5, 0.09375, ((0, 2), (2, 16)), jnp.float32),
        "block_mask": place_ends((jax.random.randint(key_list[2], (N_DEPTH, PAIRS, SUPER // BLOCK, SUPER // BLOCK), 0, 4) < 3).astype(jnp.int32), jax.random.fold_in(key_list[2], 1), 0, 1),
        "inverse_diagonal": draw_inverse_diagonal(jax.random.fold_in(key_list[4], 71), 0),
    }


def pair_offset(lower_level, upper_level):
    offset = 0
    for earlier in range(1, upper_level):
        offset = offset + earlier * 2 ** earlier
    return offset + lower_level * 2 ** upper_level


def masked_tile(factor, block_mask, device, offset):
    expand = jnp.repeat(jnp.repeat(block_mask[device, offset].astype(jnp.float32), BLOCK, axis=0), BLOCK, axis=1)
    return factor[device, offset] * expand


def product(left, right):
    return jnp.dot(left, right, precision=lax.Precision.HIGHEST, preferred_element_type=jnp.float32)


def reference(sources, factor, block_mask, inverse_diagonal):
    forward_solved = {}
    for upper_level in range(LEVELS):
        group_size = 2 ** upper_level
        for device in range(N_DEPTH):
            group_start = (device // group_size) * group_size
            position = device - group_start
            remaining = sources[device, upper_level]
            for lower_level in range(upper_level):
                offset = pair_offset(lower_level, upper_level) + position
                for member in range(group_start, group_start + group_size):
                    factor_tile = masked_tile(factor, block_mask, member, offset)
                    remaining = remaining - product(factor_tile, forward_solved[(lower_level, member)])
            forward_solved[(upper_level, device)] = product(inverse_diagonal[device, upper_level], remaining)
    backward_solved = {}
    for lower_level in reversed(range(LEVELS)):
        for device in range(N_DEPTH):
            remaining = forward_solved[(lower_level, device)]
            for upper_level in range(lower_level + 1, LEVELS):
                group_size = 2 ** upper_level
                group_start = (device // group_size) * group_size
                for position in range(group_size):
                    offset = pair_offset(lower_level, upper_level) + position
                    factor_tile = masked_tile(factor, block_mask, device, offset)
                    remaining = remaining - product(factor_tile.T, backward_solved[(upper_level, group_start + position)])
            backward_solved[(lower_level, device)] = product(inverse_diagonal[device, lower_level].T, remaining)
    return jnp.stack([jnp.stack([backward_solved[(tier_index, device)] for tier_index in range(LEVELS)]) for device in range(N_DEPTH)])
```

```python
import jax
import jax.numpy as jnp
from jax import lax
from jax.sharding import PartitionSpec as P


HIGH = lax.Precision.HIGH


def dot(left, right, contract=((1,), (0,))):
    return lax.dot_general(
        left, right, (contract, ((), ())), precision=HIGH, preferred_element_type=jnp.float32
    )


def snake(count):
    return list(range(0, count, 2)) + list(range(1, count, 2))[::-1]


def masked_share(factor, block_mask, rows_index, shots_index, shots_count):
    share, width = factor.shape[1:]
    blocks = block_mask.shape[2]
    block_size = width // blocks
    first = (rows_index * shots_count + shots_index) * share
    row_blocks = (first + jnp.arange(share, dtype=jnp.int32)) // block_size
    select = (row_blocks[:, None] == jnp.arange(blocks, dtype=jnp.int32)[None, :]).astype(jnp.float32)
    row_masks = jnp.einsum("rk,pkc->prc", select, block_mask.astype(jnp.float32), precision=lax.Precision.HIGHEST)
    expand = jnp.broadcast_to(row_masks[..., None], row_masks.shape + (block_size,))
    return factor * expand.reshape(factor.shape)


def per_device(sources, factor, block_mask, inverse_diagonal):
    shots_count = lax.axis_size("shots")
    rows_count = lax.axis_size("rows")
    depth_count = lax.axis_size("depth")
    assert rows_count == 2 and depth_count == 2 and sources.shape[1] == 2
    rows_index = lax.axis_index("rows")
    shots_index = lax.axis_index("shots")
    depth_index = lax.axis_index("depth")
    order = snake(shots_count)
    place = [order.index(index) for index in range(shots_count)]
    ahead = [(order[i], order[(i + 1) % shots_count]) for i in range(shots_count)]
    behind = [(b, a) for a, b in ahead]
    swap = [(0, 1), (1, 0)]

    tiles, share, width = factor.shape[1:]
    half = width // rows_count
    inverse0, inverse1 = inverse_diagonal[0, 0], inverse_diagonal[0, 1]
    own0, own1 = sources[0, 0], sources[0, 1]
    shots = own0.shape[1]

    def over_rows(value):
        return lax.ppermute(value, "rows", swap)

    def over_depth(value):
        return lax.ppermute(value, "depth", swap)

    masked = masked_share(factor[0], block_mask[0], rows_index, shots_index, shots_count)
    chains = {}
    for tile in range(tiles):
        chains[tile, 0] = dot(masked[tile], inverse0)
    for tile in range(tiles):
        chains[tile, 1] = dot(over_rows(masked[tile]), inverse0)

    held = []
    for key, block in chains.items():
        held.append((key, 0, block))
    forward, backward = dict(chains), dict(chains)
    hops = shots_count // 2
    for hop in range(1, hops):
        for key in chains:
            forward[key] = lax.ppermute(forward[key], "shots", ahead)
            held.append((key, -hop, forward[key]))
            backward[key] = lax.ppermute(backward[key], "shots", behind)
            held.append((key, hop, backward[key]))
    for number, key in enumerate(chains):
        if number % 2 == 0:
            held.append((key, -hops, lax.ppermute(forward[key], "shots", ahead)))
        else:
            held.append((key, hops, lax.ppermute(backward[key], "shots", behind)))

    def row_start(key, distance):
        table = jnp.array([order[(place[i] + distance) % shots_count] for i in range(shots_count)], jnp.int32)
        group = rows_index if key[1] == 0 else 1 - rows_index
        return group * half + table[shots_index] * share

    part0 = dot(inverse0, own0)
    low0 = part0[half:]
    low0 = low0 + over_rows(low0)
    base0 = dot(inverse0, jnp.concatenate([part0[:half], low0]), ((0,), (0,)))

    lower = inverse1[half:]
    other = over_rows(lower)
    near1 = dot(inverse1, inverse1, ((0,), (0,)))
    far1 = dot(lower, other, ((0,), (0,)))

    sums = [jnp.zeros((width, shots), jnp.float32) for _ in range(tiles)]
    for key, distance, block in held:
        sums[key[0]] = lax.dynamic_update_slice(sums[key[0]], dot(block, own0), (row_start(key, distance), 0))
    mine = jnp.where(depth_index == 0, sums[0], sums[1])
    theirs = jnp.where(depth_index == 0, sums[1], sums[0])
    mine = mine + over_depth(theirs)
    mine = mine + over_rows(mine)
    near = own1 - lax.dynamic_slice(mine, (rows_index * half, 0), (half, shots))
    far = over_rows(own1) - lax.dynamic_slice(mine, ((1 - rows_index) * half, 0), (half, shots))
    top = dot(near1, near) + dot(far1, far)
    top_far = over_rows(top)
    whole = jnp.concatenate(
        [jnp.where(rows_index == 0, top, top_far), jnp.where(rows_index == 0, top_far, top)]
    )
    peer = over_depth(whole)
    tops = [jnp.where(depth_index == 0, whole, peer), jnp.where(depth_index == 0, peer, whole)]
    parts = [lax.dynamic_slice(tops[key[0]], (row_start(key, distance), 0), (share, shots)) for key, distance, _ in held]
    coupling = dot(jnp.concatenate([block for _, _, block in held]), jnp.concatenate(parts), ((0,), (0,)))
    return jnp.stack([base0 - coupling, top])[None]


def solution(mesh):
    placed = (
        P("depth", None, "rows", "shots"),
        P("depth", None, ("rows", "shots"), None),
        P("depth", None, None, None),
        P("depth", None, None, "rows"),
    )
    return jax.shard_map(
        per_device,
        mesh=mesh,
        in_specs=placed,
        out_specs=P("depth", None, "rows", "shots"),
        check_vma=False,
    )
```

```python
import functools

import jax
import jax.numpy as jnp
from jax import lax
from jax.experimental import pallas as pl
from jax.experimental.pallas import tpu as pltpu
from jax.sharding import PartitionSpec as P


F32, BF16 = jnp.float32, jnp.bfloat16
VMEM = pl.BlockSpec(memory_space=pltpu.VMEM)
SMEM = pl.BlockSpec(memory_space=pltpu.SMEM)


def split(value):
    high = value.astype(BF16)
    return high, (value - high.astype(F32)).astype(BF16)


def beside(value):
    return jnp.concatenate(split(value), axis=1)


def mm(left, right, contract=((1,), (0,))):
    return lax.dot_general(left, right, (contract, ((), ())), preferred_element_type=F32)


def folded(left_high, left_low, right_pair, contract=((1,), (0,))):
    both = mm(left_high, right_pair, contract) + mm(left_low, right_pair, contract)
    width = both.shape[1] // 2
    return both[:, :width] + both[:, width:]


def call(body, outs, ins, flops, scratch=(), name=None):
    moved = sum(x.size * x.dtype.itemsize for x in ins)
    return pl.pallas_call(
        body,
        out_shape=[jax.ShapeDtypeStruct(shape, kind) for shape, kind in outs],
        in_specs=[SMEM if x.dtype == jnp.int32 else VMEM for x in ins],
        out_specs=[VMEM] * len(outs),
        scratch_shapes=list(scratch),
        name=name,
        cost_estimate=pl.CostEstimate(flops=flops, bytes_accessed=moved, transcendentals=0),
    )(*ins)


def product_body(tiles, share, block, where, mask, factor, high, low, *outs):
    width = factor.shape[2]
    parts = []
    for tile in range(tiles):
        bands = []
        for band in range(max(1, share // block)):
            rows = min(share, block)
            row_block = where[0] + band
            pieces = []
            for column in range(width // block):
                keep = mask[tile, row_block, column].astype(F32)
                pieces.append(
                    factor[tile, band * rows : (band + 1) * rows, column * block : (column + 1) * block] * keep
                )
            bands.append(jnp.concatenate(pieces, axis=1))
        parts.append(jnp.concatenate(bands, axis=0) if len(bands) > 1 else bands[0])
    rows = jnp.concatenate(parts, axis=0)
    stacked = jnp.concatenate(split(rows), axis=0)
    both = mm(stacked, high[...]) + mm(stacked, low[...])
    total = both[: tiles * share] + both[tiles * share :]
    for tile in range(tiles):
        outs[tile][...] = total[tile * share : (tile + 1) * share]


def first_body(tiles, share, block, where, mask, factor, inverse, own, *outs):
    high, low, pair = outs[tiles:]
    high[...], low[...] = split(inverse[...])
    pair[...] = beside(own[...])
    product_body(tiles, share, block, where, mask, factor, high, low, *outs[:tiles])


def hop_body(tiles, share, distances, where, spots, pair, level, *refs):
    count = len(distances)
    chunks, outs = refs[: 2 * count * tiles], refs[2 * count * tiles :]
    mine, theirs = outs[:2]
    flip = where[0]
    zero = where[1] == 0
    rhs = pair[...]
    for group in range(2):
        block = jnp.concatenate(
            [chunks[(group * count + i) * tiles + t][...] for i in range(count) for t in range(tiles)], axis=0
        )
        flat = jnp.transpose(block)
        outs[2 + 2 * group][...], outs[3 + 2 * group][...] = split(flat)
        high, low = split(block)
        value = folded(high, low, rhs)
        whole = jnp.where(flip == 0, group, 1 - group)
        for i in range(count):
            first = value[(i * tiles) * share : (i * tiles + 1) * share]
            second = value[(i * tiles + 1) * share : (i * tiles + 2) * share]
            near = -jnp.where(zero, first, second)
            if group == 0:
                near = near + level[pl.ds(pl.multiple_of(spots[i] * share, share), share), :]
            at = pl.multiple_of((i * 2 + whole) * share, share)
            mine[pl.ds(at, share), :] = near
            theirs[pl.ds(at, share), :] = -jnp.where(zero, second, first)


def start_body(high, low, pair, out):
    out[...] = folded(high[...], low[...], pair[...])


def base_body(high, low, part, far, out):
    half = far.shape[0]
    value = jnp.concatenate([part[:half, :], part[half:, :] + far[...]], axis=0)
    out[...] = folded(high[...], low[...], beside(value), ((0,), (0,)))


def square_body(inverse, other, near_high, near_low, far_high, far_low):
    half = other.shape[0]
    high, low = split(inverse[...])
    zero = ((0,), (0,))
    near = mm(high, high, zero) + mm(high, low, zero) + mm(low, high, zero)
    near_high[...], near_low[...] = split(near)
    other_high, other_low = split(other[...])
    low_high, low_low = high[half:], low[half:]
    far = mm(low_high, other_high, zero) + mm(low_high, other_low, zero) + mm(low_low, other_high, zero)
    far_high[...], far_low[...] = split(far)


def top_body(share, counts, where, spots, near_high, near_low, far_high, far_low, *refs):
    batches = len(counts)
    sums, others, out, rest = refs[:batches], refs[batches : 2 * batches], refs[2 * batches], refs[2 * batches + 1]
    half = rest.shape[1]
    place = 0
    for number, count in enumerate(counts):
        for i in range(count):
            for group in range(2):
                rows = pl.ds((i * 2 + group) * share, share)
                at = pl.multiple_of(spots[place + i] * share, share)
                rest[group, pl.ds(at, share), :] = sums[number][rows, :] + others[number][rows, :]
        place += count
    own, opposite = rest[where[0]], rest[1 - where[0]]
    out[...] = folded(near_high[...], near_low[...], beside(own)) + folded(
        far_high[...], far_low[...], beside(opposite)
    )


def couple_body(tiles, share, counts, where, spots, start, mine, peer, *refs):
    batches = len(counts)
    flats, out, both = refs[: 2 * batches], refs[2 * batches], refs[2 * batches + 1]
    both[where[1]] = mine[...]
    both[1 - where[1]] = peer[...]
    total = start[...]
    place = 0
    for number, count in enumerate(counts):
        rows = jnp.concatenate(
            [
                both[t, pl.ds(pl.multiple_of(spots[place + i] * share, share), share), :]
                for i in range(count)
                for t in range(tiles)
            ],
            axis=0,
        )
        total = total - folded(flats[2 * number][...], flats[2 * number + 1][...], beside(rows))
        place += count
    out[...] = total


def final_body(tiles, share, counts, where, spots, start, mine, peer, top, *refs):
    batches = len(counts)
    out = refs[2 * batches]
    inner = refs[: 2 * batches] + (out.at[0, 0],) + refs[2 * batches + 1 :]
    couple_body(tiles, share, counts, where, spots, start, mine, peer, *inner)
    out[0, 1] = top[...]


def snake(count):
    return list(range(0, count, 2)) + list(range(1, count, 2))[::-1]


def per_device(sources, factor, block_mask, inverse_diagonal):
    shots_count = lax.axis_size("shots")
    rows_count = lax.axis_size("rows")
    depth_count = lax.axis_size("depth")
    assert rows_count == 2 and depth_count == 2 and sources.shape[1] == 2
    rows_index = lax.axis_index("rows")
    shots_index = lax.axis_index("shots")
    depth_index = lax.axis_index("depth")
    order = snake(shots_count)
    place = [order.index(index) for index in range(shots_count)]
    ahead = [(order[i], order[(i + 1) % shots_count]) for i in range(shots_count)]
    behind = [(b, a) for a, b in ahead]
    swap = [(0, 1), (1, 0)]

    tiles, share, width = factor.shape[1:]
    half = width // rows_count
    block = width // block_mask.shape[3]
    inverse0, inverse1 = inverse_diagonal[0, 0], inverse_diagonal[0, 1]
    own0, own1 = sources[0, 0], sources[0, 1]
    shots = own0.shape[1]
    where = jnp.stack([rows_index, depth_index]).astype(jnp.int32)

    def over_rows(value):
        return lax.ppermute(value, "rows", swap)

    def over_depth(value):
        return lax.ppermute(value, "depth", swap)

    def row_block(group):
        return (((group * shots_count + shots_index) * share) // block).astype(jnp.int32)[None]

    mask = block_mask[0]
    far_factor = over_rows(factor[0])
    heavy = 8 * tiles * share * width * half
    product_outs = [((share, half), F32)] * tiles
    *chains, high0, low0, pair0 = call(
        functools.partial(first_body, tiles, share, block),
        product_outs + [((width, half), BF16)] * 2 + [((half, 2 * shots), BF16)],
        [row_block(rows_index), mask, factor[0], inverse0, own0],
        heavy,
        name="first",
    )
    chains += call(
        functools.partial(product_body, tiles, share, block),
        product_outs,
        [row_block(1 - rows_index), mask, far_factor, high0, low0],
        heavy,
        name="second",
    )

    hops = shots_count // 2
    stages = [([0], [[piece] for piece in chains])]
    forward, backward = list(chains), list(chains)
    for hop in range(1, hops):
        for number in range(len(chains)):
            forward[number] = lax.ppermute(forward[number], "shots", ahead)
            backward[number] = lax.ppermute(backward[number], "shots", behind)
        stages.append(([-hop, hop], [list(pieces) for pieces in zip(forward, backward)]))
    final = []
    for number in range(len(chains)):
        if number % 2 == 0:
            final.append([lax.ppermute(forward[number], "shots", ahead)])
        else:
            final.append([lax.ppermute(backward[number], "shots", behind)])
    stages.append(([hops], final))

    def spot(distance):
        table = jnp.array([order[(place[i] + distance) % shots_count] for i in range(shots_count)], jnp.int32)
        return table[shots_index]

    (part0,) = call(start_body, [((width, shots), F32)], [high0, low0, pair0], 8 * width * half * shots, name="start")
    far0 = over_rows(part0[half:])
    (base0,) = call(
        base_body, [((half, shots), F32)], [high0, low0, part0, far0], 8 * width * half * shots, name="base"
    )

    other1 = over_rows(inverse1[half:])
    squares = call(
        square_body, [((half, half), BF16)] * 4, [inverse1, other1], 9 * half * half * half * 2, name="square"
    )

    sums, others, flats, counts, spots = [], [], [[], []], [], []
    for distances, pieces in stages:
        count = len(distances)
        marks = jnp.stack([spot(distance) for distance in distances])
        ordered = [pieces[group * tiles + t][i] for group in range(2) for i in range(count) for t in range(tiles)]
        deep = count * tiles * share
        mine, theirs, *flat = call(
            functools.partial(hop_body, tiles, share, distances),
            [((2 * count * share, shots), F32)] * 2 + [((half, deep), BF16)] * 4,
            [where, marks, pair0, own1] + ordered,
            16 * deep * half * shots,
            name="hop",
        )
        total = mine + over_depth(theirs)
        sums.append(total)
        others.append(over_rows(total))
        flats[0] += flat[:2]
        flats[1] += flat[2:]
        counts.append(count)
        spots.append(marks)
    spots = jnp.concatenate(spots)

    (top,) = call(
        functools.partial(top_body, share, counts),
        [((half, shots), F32)],
        [where, spots, *squares, *sums, *others],
        16 * half * half * shots,
        scratch=[pltpu.VMEM((2, half, shots), F32)],
        name="top",
    )
    far_top = over_rows(top)
    peer_top = over_depth(top)
    peer_far = over_depth(far_top)
    work = 8 * half * width * shots
    (almost,) = call(
        functools.partial(couple_body, tiles, share, counts),
        [((half, shots), F32)],
        [where, spots, base0, top, peer_top, *flats[0]],
        work,
        scratch=[pltpu.VMEM((2, half, shots), F32)],
        name="couple",
    )
    (answer,) = call(
        functools.partial(final_body, tiles, share, counts),
        [((1, 2, half, shots), F32)],
        [where, spots, almost, far_top, peer_far, top, *flats[1]],
        work,
        scratch=[pltpu.VMEM((2, half, shots), F32)],
        name="final",
    )
    return answer


def solution(mesh):
    placed = (
        P("depth", None, "rows", "shots"),
        P("depth", None, ("rows", "shots"), None),
        P("depth", None, None, None),
        P("depth", None, None, "rows"),
    )
    return jax.shard_map(
        per_device,
        mesh=mesh,
        in_specs=placed,
        out_specs=P("depth", None, "rows", "shots"),
        check_vma=False,
    )
```

```python
import functools

import jax
import jax.numpy as jnp
from jax import lax
from jax.experimental import pallas as pl
from jax.experimental.pallas import tpu as pltpu
from jax.sharding import PartitionSpec as P


F32, BF16 = jnp.float32, jnp.bfloat16
VMEM = pl.BlockSpec(memory_space=pltpu.VMEM)
SMEM = pl.BlockSpec(memory_space=pltpu.SMEM)
GRANT = 12 * 1024 * 1024


def split(value):
    high = value.astype(BF16)
    return high, (value - high.astype(F32)).astype(BF16)


def beside(value):
    return jnp.concatenate(split(value), axis=1)


def mm(left, right, contract=((1,), (0,))):
    return lax.dot_general(left, right, (contract, ((), ())), preferred_element_type=F32)


def folded(left_high, left_low, right_pair, contract=((1,), (0,))):
    both = mm(left_high, right_pair, contract) + mm(left_low, right_pair, contract)
    width = both.shape[1] // 2
    return both[:, :width] + both[:, width:]


def level_of(array, level):
    return array, level


def call(body, outs, ins, flops, scratch=(), name=None):
    arrays = [x[0] if isinstance(x, tuple) else x for x in ins]
    levels = [x[1] if isinstance(x, tuple) else None for x in ins]
    picked = [i for i, level in enumerate(levels) if level is not None]

    def specs(array, level):
        if level is not None:
            return pl.BlockSpec(memory_space=pl.ANY)
        return SMEM if array.dtype == jnp.int32 else VMEM

    def run(*refs):
        refs = list(refs)
        if picked:
            semaphores = refs.pop()
            buffers = [refs.pop() for _ in picked][::-1]
            copies = []
            for number, i in enumerate(picked):
                source = refs[i].at[0, levels[i]]
                copies.append(pltpu.make_async_copy(source, buffers[number], semaphores.at[number]))
                copies[-1].start()
                refs[i] = buffers[number]
            for copy in copies:
                copy.wait()
        body(*refs)

    held = [pltpu.VMEM(arrays[i].shape[2:], arrays[i].dtype) for i in picked]
    if picked:
        held.append(pltpu.SemaphoreType.DMA((len(picked),)))
    moved = sum(x.size * x.dtype.itemsize for x in arrays)
    return pl.pallas_call(
        run,
        out_shape=[jax.ShapeDtypeStruct(shape, kind) for shape, kind in outs],
        in_specs=[specs(array, level) for array, level in zip(arrays, levels)],
        out_specs=[VMEM] * len(outs),
        scratch_shapes=list(scratch) + held,
        name=name,
        compiler_params=pltpu.CompilerParams(vmem_limit_bytes=GRANT),
        cost_estimate=pl.CostEstimate(flops=flops, bytes_accessed=moved, transcendentals=0),
    )(*arrays)


def spot(distance):
    count, index = lax.axis_size("shots"), lax.axis_index("shots")
    at = lax.rem(jnp.where(index % 2 == 0, index // 2, count - 1 - index // 2) + (distance + count), count)
    return jnp.where(2 * at < count, 2 * at, 2 * (count - 1 - at) + 1)


def share_rows(distance, share):
    return pl.ds(pl.multiple_of(spot(distance) * share, share), share)


def product(tiles, share, block, group, mask, factor, high, low, outs):
    width = high.shape[0]
    first = ((group * lax.axis_size("shots") + lax.axis_index("shots")) * share) // block
    size = min(share, block)
    parts = []
    for tile in range(tiles):
        for band in range(share // size):
            pieces = []
            for column in range(width // block):
                keep = mask[0, tile, first + band, column].astype(F32)
                pieces.append(factor(tile, slice(band * size, (band + 1) * size), column * block, block) * keep)
            parts.append(jnp.concatenate(pieces, axis=1))
    stacked = jnp.concatenate(split(jnp.concatenate(parts, axis=0)), axis=0)
    both = mm(stacked, high[...]) + mm(stacked, low[...])
    total = both[: tiles * share] + both[tiles * share :]
    for tile in range(tiles):
        outs[tile][...] = total[tile * share : (tile + 1) * share]


def first_body(tiles, share, block, mask, factor, inverse, own, *outs):
    high, low, pair = outs[tiles:]
    high[...], low[...] = split(inverse[...])
    pair[...] = beside(own[...])

    def load(tile, rows, start, size):
        return factor[0, tile, rows, start : start + size]

    product(tiles, share, block, lax.axis_index("rows"), mask, load, high, low, outs[:tiles])


def second_body(tiles, share, block, mask, left, right, high, low, inverse, *outs):
    half = left.shape[2]
    quarter = half // 2
    one, two, three, four = outs[tiles:]
    one[...] = inverse[half : half + quarter, :quarter]
    two[...] = inverse[half + quarter :, :quarter]
    three[...] = inverse[half + quarter :, quarter:]
    four[...] = inverse[half : half + quarter, quarter:]

    def load(tile, rows, start, size):
        side = left if start < half else right
        return side[tile, rows, start % half : start % half + size]

    product(tiles, share, block, 1 - lax.axis_index("rows"), mask, load, high, low, outs[:tiles])


def hop_body(tiles, share, distances, pair, level, *refs):
    count = len(distances)
    chunks, outs = refs[: 2 * count * tiles], refs[2 * count * tiles :]
    mine, theirs = outs[:2]
    flip, zero = lax.axis_index("rows"), lax.axis_index("depth") == 0
    rhs = pair[...]
    for group in range(2):
        block = jnp.concatenate(
            [chunks[(group * count + i) * tiles + t][...] for i in range(count) for t in range(tiles)], axis=0
        )
        outs[2 + 2 * group][...], outs[3 + 2 * group][...] = split(jnp.transpose(block))
        value = folded(*split(block), rhs)
        half_index = jnp.where(flip == 0, group, 1 - group)
        for i in range(count):
            first = value[(i * tiles) * share : (i * tiles + 1) * share]
            second = value[(i * tiles + 1) * share : (i * tiles + 2) * share]
            near = -jnp.where(zero, first, second)
            if group == 0:
                near = near + level[share_rows(distances[i], share), :]
            at = pl.ds(pl.multiple_of((i * 2 + half_index) * share, share), share)
            mine[at, :] = near
            theirs[at, :] = -jnp.where(zero, second, first)


def start_body(high, low, pair, out, lower):
    value = folded(high[...], low[...], pair[...])
    out[...] = value
    lower[...] = value[value.shape[0] // 2 :]


def base_body(high, low, part, far, out):
    half = far.shape[0]
    value = jnp.concatenate([part[:half, :], part[half:, :] + far[...]], axis=0)
    rows = jnp.concatenate(split(jnp.transpose(value)), axis=0)
    both = mm(rows, high[...]) + mm(rows, low[...])
    shots = both.shape[0] // 2
    out[...] = jnp.transpose(both[:shots] + both[shots:])


def square_body(inverse, one, two, three, four, near_high, near_low, far_high, far_low):
    half = inverse.shape[1]
    high, low = split(inverse[...])
    turned_high, turned_low = jnp.transpose(high), jnp.transpose(low)
    near = mm(turned_high, high) + mm(turned_high, low) + mm(turned_low, high)
    near_high[...], near_low[...] = split(near)
    other = jnp.concatenate(
        [jnp.concatenate([one[...], four[...]], axis=1), jnp.concatenate([two[...], three[...]], axis=1)], axis=0
    )
    other_high, other_low = split(other)
    turned_high, turned_low = turned_high[:, half:], turned_low[:, half:]
    far = mm(turned_high, other_high) + mm(turned_high, other_low) + mm(turned_low, other_high)
    far_high[...], far_low[...] = split(far)


def top_body(share, stages, near_high, near_low, far_high, far_low, *refs):
    batches = len(stages)
    sums, others, out, rest = refs[:batches], refs[batches : 2 * batches], refs[2 * batches], refs[2 * batches + 1]
    for number, distances in enumerate(stages):
        for i, distance in enumerate(distances):
            for group in range(2):
                rows = pl.ds((i * 2 + group) * share, share)
                rest[group, share_rows(distance, share), :] = sums[number][rows, :] + others[number][rows, :]
    flip = lax.axis_index("rows")
    out[...] = folded(near_high[...], near_low[...], beside(rest[flip])) + folded(
        far_high[...], far_low[...], beside(rest[1 - flip])
    )


def couple(tiles, share, stages, start, mine, peer, flats, both):
    depth = lax.axis_index("depth")
    both[depth] = mine[...]
    both[1 - depth] = peer[...]
    rows = [
        jnp.concatenate(
            [both[t, share_rows(distance, share), :] for distance in distances for t in range(tiles)], axis=0
        )
        for distances in stages
    ]
    highs, lows = [flat[...] for flat in flats[::2]], [flat[...] for flat in flats[1::2]]
    if all(flat.shape[1] % 128 == 0 for flat in highs):
        rows = [jnp.concatenate(rows, axis=0)]
        highs, lows = [jnp.concatenate(highs, axis=1)], [jnp.concatenate(lows, axis=1)]
    total = start[...]
    for high, low, row in zip(highs, lows, rows):
        total = total - folded(high, low, beside(row))
    return total


def couple_body(tiles, share, stages, start, mine, peer, *refs):
    *flats, out, both = refs
    out[...] = couple(tiles, share, stages, start, mine, peer, flats, both)


def final_body(tiles, share, stages, start, mine, peer, top, *refs):
    *flats, out, both = refs
    out[0, 1] = top[...]
    out[0, 0] = couple(tiles, share, stages, start, mine, peer, flats, both)


def snake(count):
    return list(range(0, count, 2)) + list(range(1, count, 2))[::-1]


def per_device(sources, factor, block_mask, inverse_diagonal):
    shots_count = lax.axis_size("shots")
    rows_count = lax.axis_size("rows")
    depth_count = lax.axis_size("depth")
    assert rows_count == 2 and depth_count == 2 and sources.shape[1] == 2 and shots_count % 2 == 0
    order = snake(shots_count)
    ahead = [(order[i], order[(i + 1) % shots_count]) for i in range(shots_count)]
    behind = [(b, a) for a, b in ahead]
    swap = [(0, 1), (1, 0)]

    tiles, share, width = factor.shape[1:]
    half = width // rows_count
    block = width // block_mask.shape[3]
    shots = sources.shape[3]
    quarter = half // 2

    def over_rows(value, pairs=swap):
        return lax.ppermute(value, "rows", pairs)

    def over_depth(value):
        return lax.ppermute(value, "depth", swap)

    far_right = over_rows(factor[0, :, :, half:])
    far_left = over_rows(factor[0, :, :, :half], [(1, 0)])
    heavy = 8 * tiles * share * width * half
    product_outs = [((share, half), F32)] * tiles
    *chains, high0, low0, pair0 = call(
        functools.partial(first_body, tiles, share, block),
        product_outs + [((width, half), BF16)] * 2 + [((half, 2 * shots), BF16)],
        [block_mask, factor, level_of(inverse_diagonal, 0), level_of(sources, 0)],
        heavy,
        name="first",
    )
    *more, one, two, three, four = call(
        functools.partial(second_body, tiles, share, block),
        product_outs + [((quarter, quarter), F32)] * 4,
        [block_mask, far_left, far_right, high0, low0, level_of(inverse_diagonal, 1)],
        heavy,
        name="second",
    )
    chains += more

    hops = shots_count // 2
    stages, pieces = [[0]], [[[piece] for piece in chains]]
    forward, backward = list(chains), list(chains)
    for hop in range(1, hops):
        for number in range(len(chains)):
            forward[number] = lax.ppermute(forward[number], "shots", ahead)
            backward[number] = lax.ppermute(backward[number], "shots", behind)
        stages.append([-hop, hop])
        pieces.append([list(pair) for pair in zip(forward, backward)])
    stages.append([hops])
    pieces.append(
        [
            [lax.ppermute(forward[number], "shots", ahead) if number % 2 == 0 else lax.ppermute(backward[number], "shots", behind)]
            for number in range(len(chains))
        ]
    )

    part0, lower0 = call(
        start_body,
        [((width, shots), F32), ((half, shots), F32)],
        [high0, low0, pair0],
        8 * width * half * shots,
        name="start",
    )
    far0 = over_rows(lower0)
    (base0,) = call(
        base_body, [((half, shots), F32)], [high0, low0, part0, far0], 8 * width * half * shots, name="base"
    )

    others1 = [over_rows(one), over_rows(two), over_rows(three), over_rows(four, [(0, 1)])]
    squares = call(
        square_body,
        [((half, half), BF16)] * 4,
        [level_of(inverse_diagonal, 1), *others1],
        9 * half * half * half * 2,
        name="square",
    )

    sums, others, flats = [], [], [[], []]
    for distances, piece in zip(stages, pieces):
        count = len(distances)
        ordered = [piece[group * tiles + t][i] for group in range(2) for i in range(count) for t in range(tiles)]
        deep = count * tiles * share
        mine, theirs, *flat = call(
            functools.partial(hop_body, tiles, share, distances),
            [((2 * count * share, shots), F32)] * 2 + [((half, deep), BF16)] * 4,
            [pair0, level_of(sources, 1)] + ordered,
            16 * deep * half * shots,
            name="hop",
        )
        total = mine + over_depth(theirs)
        sums.append(total)
        others.append(over_rows(total))
        flats[0] += flat[:2]
        flats[1] += flat[2:]

    (top,) = call(
        functools.partial(top_body, share, stages),
        [((half, shots), F32)],
        [*squares, *sums, *others],
        16 * half * half * shots,
        scratch=[pltpu.VMEM((2, half, shots), F32)],
        name="top",
    )
    far_top = over_rows(top)
    peer_top = over_depth(top)
    peer_far = over_depth(far_top)
    work = 8 * half * width * shots
    (almost,) = call(
        functools.partial(couple_body, tiles, share, stages),
        [((half, shots), F32)],
        [base0, top, peer_top, *flats[0]],
        work,
        scratch=[pltpu.VMEM((2, half, shots), F32)],
        name="couple",
    )
    (answer,) = call(
        functools.partial(final_body, tiles, share, stages),
        [((1, 2, half, shots), F32)],
        [almost, far_top, peer_far, top, *flats[1]],
        work,
        scratch=[pltpu.VMEM((2, half, shots), F32)],
        name="final",
    )
    return answer


def solution(mesh):
    placed = (
        P("depth", None, "rows", "shots"),
        P("depth", None, ("rows", "shots"), None),
        P("depth", None, None, None),
        P("depth", None, None, "rows"),
    )
    return jax.shard_map(
        per_device,
        mesh=mesh,
        in_specs=placed,
        out_specs=P("depth", None, "rows", "shots"),
        check_vma=False,
    )
```

```python
import functools

import jax
import jax.numpy as jnp
from jax import lax
from jax.experimental import pallas as pl
from jax.experimental.pallas import tpu as pltpu
from jax.sharding import PartitionSpec as P


F32, BF16 = jnp.float32, jnp.bfloat16
VMEM = pl.BlockSpec(memory_space=pltpu.VMEM)
SMEM = pl.BlockSpec(memory_space=pltpu.SMEM)
GRANT = 12 * 1024 * 1024


def split(value):
    high = value.astype(BF16)
    return high, (value - high.astype(F32)).astype(BF16)


def beside(value):
    return jnp.concatenate(split(value), axis=1)


def mm(left, right, contract=((1,), (0,))):
    return lax.dot_general(left, right, (contract, ((), ())), preferred_element_type=F32)


def folded(left_high, left_low, right_pair, contract=((1,), (0,))):
    both = mm(left_high, right_pair, contract) + mm(left_low, right_pair, contract)
    width = both.shape[1] // 2
    return both[:, :width] + both[:, width:]


def part_of(array, *index):
    return array, index


def call(body, outs, ins, flops, scratch=()):
    arrays = [x[0] if isinstance(x, tuple) else x for x in ins]
    parts = [x[1] if isinstance(x, tuple) else None for x in ins]
    picked = [i for i, index in enumerate(parts) if index is not None]

    def specs(array, index):
        if index is not None:
            return pl.BlockSpec(memory_space=pltpu.HBM)
        return SMEM if array.dtype == jnp.int32 else VMEM

    def run(*refs):
        refs = list(refs)
        if picked:
            semaphores = refs.pop()
            buffers = [refs.pop() for _ in picked][::-1]
            copies = []
            for number, i in enumerate(picked):
                source = refs[i].at[parts[i]]
                copies.append(pltpu.make_async_copy(source, buffers[number], semaphores.at[number]))
                copies[-1].start()
                refs[i] = buffers[number]
            for copy in copies:
                copy.wait()
        body(*refs)

    held = [pltpu.VMEM(arrays[i].shape[len(parts[i]) :], arrays[i].dtype) for i in picked]
    if picked:
        held.append(pltpu.SemaphoreType.DMA((len(picked),)))
    moved = sum(x.size * x.dtype.itemsize for x in arrays)
    return pl.pallas_call(
        run,
        out_shape=[jax.ShapeDtypeStruct(shape, kind) for shape, kind in outs],
        in_specs=[specs(array, index) for array, index in zip(arrays, parts)],
        out_specs=[VMEM] * len(outs),
        scratch_shapes=list(scratch) + held,
        compiler_params=pltpu.CompilerParams(vmem_limit_bytes=GRANT),
        cost_estimate=pl.CostEstimate(flops=flops, bytes_accessed=moved, transcendentals=0),
    )(*arrays)


def spot(distance):
    count, index = lax.axis_size("shots"), lax.axis_index("shots")
    at = lax.rem(jnp.where(index % 2 == 0, index // 2, count - 1 - index // 2) + (distance + count), count)
    return jnp.where(2 * at < count, 2 * at, 2 * (count - 1 - at) + 1)


def share_rows(distance, share):
    return pl.ds(pl.multiple_of(spot(distance) * share, share), share)


def product(tiles, share, block, group, mask, factor, high, low, out):
    width = high.shape[0]
    first = ((group * lax.axis_size("shots") + lax.axis_index("shots")) * share) // block
    size = min(share, block)
    parts = []
    for tile in range(tiles):
        for band in range(share // size):
            pieces = []
            for column in range(width // block):
                keep = mask[0, tile, first + band, column].astype(F32)
                pieces.append(factor(tile, slice(band * size, (band + 1) * size), column * block, block) * keep)
            parts.append(jnp.concatenate(pieces, axis=1))
    stacked = jnp.concatenate(split(jnp.concatenate(parts, axis=0)), axis=0)
    both = mm(stacked, high[...]) + mm(stacked, low[...])
    out[...] = both[: tiles * share] + both[tiles * share :]


def first_body(tiles, share, block, mask, factor, inverse, own, out, high, low, pair):
    high[...], low[...] = split(inverse[...])
    pair[...] = beside(own[...])

    def load(tile, rows, start, size):
        return factor[tile, rows, start : start + size]

    product(tiles, share, block, lax.axis_index("rows"), mask, load, high, low, out)


def second_body(tiles, share, block, mask, left, right, high, low, inverse, out, three, corner):
    half = left.shape[2]
    quarter = half // 2
    three[0] = inverse[half : half + quarter, :quarter]
    three[1] = inverse[half + quarter :, :quarter]
    three[2] = inverse[half + quarter :, quarter:]
    corner[...] = inverse[half : half + quarter, quarter:]

    def load(tile, rows, start, size):
        side = left if start < half else right
        return side[tile, rows, start % half : start % half + size]

    product(tiles, share, block, 1 - lax.axis_index("rows"), mask, load, high, low, out)


def hop_body(tiles, share, distances, pair, level, *refs):
    count = len(distances)
    chunks, outs = refs[: 2 * count], refs[2 * count :]
    mine, theirs = outs[:2]
    flip, zero = lax.axis_index("rows"), lax.axis_index("depth") == 0
    rhs = pair[...]
    for group in range(2):
        block = jnp.concatenate([chunks[group * count + i][...] for i in range(count)], axis=0)
        outs[2 + 2 * group][...], outs[3 + 2 * group][...] = split(jnp.transpose(block))
        value = folded(*split(block), rhs)
        half_index = jnp.where(flip == 0, group, 1 - group)
        for i in range(count):
            first = value[(i * tiles) * share : (i * tiles + 1) * share]
            second = value[(i * tiles + 1) * share : (i * tiles + 2) * share]
            near = -jnp.where(zero, first, second)
            if group == 0:
                near = near + level[share_rows(distances[i], share), :]
            at = pl.ds(pl.multiple_of((i * 2 + half_index) * share, share), share)
            mine[at, :] = near
            theirs[at, :] = -jnp.where(zero, second, first)


def start_body(high, low, pair, out, lower):
    value = folded(high[...], low[...], pair[...])
    out[...] = value
    lower[...] = value[value.shape[0] // 2 :]


def base_body(high, low, part, far, out):
    half = far.shape[0]
    value = jnp.concatenate([part[:half, :], part[half:, :] + far[...]], axis=0)
    rows = jnp.concatenate(split(jnp.transpose(value)), axis=0)
    both = mm(rows, high[...]) + mm(rows, low[...])
    shots = both.shape[0] // 2
    out[...] = jnp.transpose(both[:shots] + both[shots:])


def square_body(inverse, three, corner, near_high, near_low, far_high, far_low):
    half = inverse.shape[1]
    high, low = split(inverse[...])
    turned_high, turned_low = jnp.transpose(high), jnp.transpose(low)
    near = mm(turned_high, high) + mm(turned_high, low) + mm(turned_low, high)
    near_high[...], near_low[...] = split(near)
    other = jnp.concatenate(
        [jnp.concatenate([three[0], corner[...]], axis=1), jnp.concatenate([three[1], three[2]], axis=1)], axis=0
    )
    other_high, other_low = split(other)
    turned_high, turned_low = turned_high[:, half:], turned_low[:, half:]
    far = mm(turned_high, other_high) + mm(turned_high, other_low) + mm(turned_low, other_high)
    far_high[...], far_low[...] = split(far)


def top_body(share, stages, near_high, near_low, far_high, far_low, *refs):
    batches = len(stages)
    sums, others, out, rest = refs[:batches], refs[batches : 2 * batches], refs[2 * batches], refs[2 * batches + 1]
    for number, distances in enumerate(stages):
        for i, distance in enumerate(distances):
            for group in range(2):
                rows = pl.ds((i * 2 + group) * share, share)
                rest[group, share_rows(distance, share), :] = sums[number][rows, :] + others[number][rows, :]
    flip = lax.axis_index("rows")
    out[...] = folded(near_high[...], near_low[...], beside(rest[flip])) + folded(
        far_high[...], far_low[...], beside(rest[1 - flip])
    )


def couple(tiles, share, stages, start, mine, peer, flats, both):
    depth = lax.axis_index("depth")
    both[depth] = mine[...]
    both[1 - depth] = peer[...]
    rows = [
        jnp.concatenate(
            [both[t, share_rows(distance, share), :] for distance in distances for t in range(tiles)], axis=0
        )
        for distances in stages
    ]
    highs, lows = [flat[...] for flat in flats[::2]], [flat[...] for flat in flats[1::2]]
    if all(flat.shape[1] % 128 == 0 for flat in highs):
        rows = [jnp.concatenate(rows, axis=0)]
        highs, lows = [jnp.concatenate(highs, axis=1)], [jnp.concatenate(lows, axis=1)]
    total = start[...]
    for high, low, row in zip(highs, lows, rows):
        total = total - folded(high, low, beside(row))
    return total


def couple_body(tiles, share, stages, start, mine, peer, *refs):
    *flats, out, both = refs
    out[...] = couple(tiles, share, stages, start, mine, peer, flats, both)


def final_body(tiles, share, stages, start, mine, peer, top, *refs):
    *flats, out, both = refs
    out[0, 1] = top[...]
    out[0, 0] = couple(tiles, share, stages, start, mine, peer, flats, both)


def snake(count):
    return list(range(0, count, 2)) + list(range(1, count, 2))[::-1]


def per_device(sources, factor, block_mask, inverse_diagonal):
    shots_count = lax.axis_size("shots")
    rows_count = lax.axis_size("rows")
    depth_count = lax.axis_size("depth")
    assert rows_count == 2 and depth_count == 2 and sources.shape[1] == 2 and shots_count % 2 == 0
    order = snake(shots_count)
    ahead = [(order[i], order[(i + 1) % shots_count]) for i in range(shots_count)]
    behind = [(b, a) for a, b in ahead]
    swap = [(0, 1), (1, 0)]

    tiles, share, width = factor.shape[1:]
    half = width // rows_count
    block = width // block_mask.shape[3]
    shots = sources.shape[3]
    quarter = half // 2

    far_right = lax.ppermute(factor[0, :, :, half:], "rows", swap)
    far_left = lax.ppermute(factor[0, :, :, :half], "rows", [(1, 0)])
    heavy = 8 * tiles * share * width * half
    chunk = ((tiles * share, half), F32)
    own, high0, low0, pair0 = call(
        functools.partial(first_body, tiles, share, block),
        [chunk] + [((width, half), BF16)] * 2 + [((half, 2 * shots), BF16)],
        [block_mask, part_of(factor, 0), part_of(inverse_diagonal, 0, 0), part_of(sources, 0, 0)],
        heavy,
    )
    far, three1, corner1 = call(
        functools.partial(second_body, tiles, share, block),
        [chunk, ((3, quarter, quarter), F32), ((quarter, quarter), F32)],
        [block_mask, far_left, far_right, high0, low0, part_of(inverse_diagonal, 0, 1)],
        heavy,
    )

    hops = shots_count // 2
    stages, pieces = [[0]], [[[own], [far]]]
    forward, backward = [own, far], [own, far]
    for hop in range(1, hops):
        for number in range(2):
            forward[number] = lax.ppermute(forward[number], "shots", ahead)
            backward[number] = lax.ppermute(backward[number], "shots", behind)
        if hop == 1:
            stages[0] += [-1, 1]
            for number in range(2):
                pieces[0][number] += [forward[number], backward[number]]
        else:
            stages.append([-hop, hop])
            pieces.append([list(pair) for pair in zip(forward, backward)])
    stages.append([hops])
    pieces.append([[lax.ppermute(forward[0], "shots", ahead)], [lax.ppermute(backward[1], "shots", behind)]])

    part0, lower0 = call(
        start_body, [((width, shots), F32), ((half, shots), F32)], [high0, low0, pair0], 8 * width * half * shots
    )
    far0 = lax.ppermute(lower0, "rows", swap)
    (base0,) = call(base_body, [((half, shots), F32)], [high0, low0, part0, far0], 8 * width * half * shots)

    squares = call(
        square_body,
        [((half, half), BF16)] * 4,
        [part_of(inverse_diagonal, 0, 1), lax.ppermute(three1, "rows", swap), lax.ppermute(corner1, "rows", [(0, 1)])],
        9 * half * half * half * 2,
    )

    sums, others, flats = [], [], [[], []]
    for distances, piece in zip(stages, pieces):
        count = len(distances)
        deep = count * tiles * share
        mine, theirs, *flat = call(
            functools.partial(hop_body, tiles, share, distances),
            [((2 * count * share, shots), F32)] * 2 + [((half, deep), BF16)] * 4,
            [pair0, part_of(sources, 0, 1)] + piece[0] + piece[1],
            16 * deep * half * shots,
        )
        total = mine + lax.ppermute(theirs, "depth", swap)
        sums.append(total)
        others.append(lax.ppermute(total, "rows", swap))
        flats[0] += flat[:2]
        flats[1] += flat[2:]

    (top,) = call(
        functools.partial(top_body, share, stages),
        [((half, shots), F32)],
        [*squares, *sums, *others],
        16 * half * half * shots,
        scratch=[pltpu.VMEM((2, half, shots), F32)],
    )
    far_top = lax.ppermute(top, "rows", swap)
    peer_top = lax.ppermute(top, "depth", swap)
    peer_far = lax.ppermute(far_top, "depth", swap)
    work = 8 * half * width * shots
    (almost,) = call(
        functools.partial(couple_body, tiles, share, stages),
        [((half, shots), F32)],
        [base0, top, peer_top, *flats[0]],
        work,
        scratch=[pltpu.VMEM((2, half, shots), F32)],
    )
    (answer,) = call(
        functools.partial(final_body, tiles, share, stages),
        [((1, 2, half, shots), F32)],
        [almost, far_top, peer_far, top, *flats[1]],
        work,
        scratch=[pltpu.VMEM((2, half, shots), F32)],
    )
    return answer


def solution(mesh):
    placed = (
        P("depth", None, "rows", "shots"),
        P("depth", None, ("rows", "shots"), None),
        P("depth", None, None, None),
        P("depth", None, None, "rows"),
    )

    return jax.shard_map(
        per_device,
        mesh=mesh,
        in_specs=placed,
        out_specs=P("depth", None, "rows", "shots"),
        check_vma=False,
    )
```

```python
import functools

import jax
import jax.numpy as jnp
from jax import lax
from jax.experimental import pallas as pl
from jax.experimental.pallas import tpu as pltpu
from jax.sharding import PartitionSpec as P


F32, BF16 = jnp.float32, jnp.bfloat16
VMEM = pl.BlockSpec(memory_space=pltpu.VMEM)
HBM = pl.BlockSpec(memory_space=pltpu.HBM)
GRANT = 12 * 1024 * 1024


def split(value):
    high = value.astype(BF16)
    return high, (value - high.astype(F32)).astype(BF16)


def beside(value):
    return jnp.concatenate(split(value), axis=1)


def mm(left, right, contract=((1,), (0,))):
    return lax.dot_general(left, right, (contract, ((), ())), preferred_element_type=F32)


def folded(left_high, left_low, right_pair, contract=((1,), (0,))):
    both = mm(left_high, right_pair, contract) + mm(left_low, right_pair, contract)
    width = both.shape[1] // 2
    return both[:, :width] + both[:, width:]


def part_of(array, *index):
    return array, index


def call(body, outs, ins, flops, scratch=(), plain=(), placed=(), alias=None):
    arrays = [pltpu.with_memory_space_constraint(x[0], pltpu.HBM) if isinstance(x, tuple) else x for x in ins]
    parts = [x[1] if isinstance(x, tuple) else None for x in ins]
    picked = [i for i, index in enumerate(parts) if index is not None]

    def space(array):
        return pltpu.SMEM if array.dtype == jnp.int32 else pltpu.VMEM

    def run(*refs):
        refs = list(refs)
        if picked:
            semaphores = refs.pop()
            buffers = [refs.pop() for _ in picked][::-1]
            copies = []
            for number, i in enumerate(picked):
                source = refs[i].at[parts[i]]
                copies.append(pltpu.make_async_copy(source, buffers[number], semaphores.at[number]))
                copies[-1].start()
                refs[i] = buffers[number]
            for copy in copies:
                copy.wait()
        body(*refs)

    held = [space(arrays[i])(arrays[i].shape[len(parts[i]) :], arrays[i].dtype) for i in picked]
    if picked:
        held.append(pltpu.SemaphoreType.DMA((len(picked),)))
    moved = sum(x.size * x.dtype.itemsize for x in arrays)
    return pl.pallas_call(
        run,
        out_shape=[jax.ShapeDtypeStruct(shape, kind) for shape, kind in outs],
        in_specs=[HBM if index is not None or i in plain else VMEM for i, index in enumerate(parts)],
        out_specs=[HBM if i in placed else VMEM for i in range(len(outs))],
        scratch_shapes=list(scratch) + held,
        input_output_aliases=alias or {},
        compiler_params=pltpu.CompilerParams(vmem_limit_bytes=GRANT),
        cost_estimate=pl.CostEstimate(flops=flops, bytes_accessed=moved, transcendentals=0),
    )(*arrays)


def spot(distance):
    count, index = lax.axis_size("shots"), lax.axis_index("shots")
    at = lax.rem(jnp.where(index % 2 == 0, index // 2, count - 1 - index // 2) + (distance + count), count)
    return jnp.where(2 * at < count, 2 * at, 2 * (count - 1 - at) + 1)


def share_rows(distance, share):
    return pl.ds(pl.multiple_of(spot(distance) * share, share), share)


def product(tiles, share, block, group, mask, factor, high, low, out):
    width = high.shape[0]
    first = ((group * lax.axis_size("shots") + lax.axis_index("shots")) * share) // block
    size = min(share, block)
    parts = []
    for tile in tiles:
        for band in range(share // size):
            pieces = []
            for column in range(width // block):
                keep = mask[tile, first + band, column].astype(F32)
                pieces.append(factor(tile, slice(band * size, (band + 1) * size), column * block, block) * keep)
            parts.append(jnp.concatenate(pieces, axis=1))
    stacked = jnp.concatenate(split(jnp.concatenate(parts, axis=0)), axis=0)
    both = mm(stacked, high[...]) + mm(stacked, low[...])
    out[...] = both[: len(tiles) * share] + both[len(tiles) * share :]


def first_body(tiles, share, block, mask, factor, inverse, own, out, high, low, pair):
    high[...], low[...] = split(inverse[...])
    pair[...] = beside(own[...])

    def load(tile, rows, start, size):
        return factor[tile, rows, start : start + size]

    product(range(tiles), share, block, lax.axis_index("rows"), mask, load, high, low, out)


def second_body(tile, share, block, mask, left, right, high, low, out):
    half = left.shape[1]

    def load(_, rows, start, size):
        return left[rows, start : start + size] if start < half else right[tile, rows, start - half : start - half + size]

    product([tile], share, block, 1 - lax.axis_index("rows"), mask, load, high, low, out)


def halves_body(factor, *refs):
    *outs, semaphores = refs
    half = factor.shape[3] // 2
    sources = [factor.at[0, tile, :, :half] for tile in range(factor.shape[1])] + [factor.at[0, :, :, half:]]
    copies = [
        pltpu.make_async_copy(source, out, semaphores.at[number])
        for number, (source, out) in enumerate(zip(sources, outs))
    ]
    for copy in copies:
        copy.start()
    for copy in copies:
        copy.wait()


def hop_body(tiles, share, distances, pair, level, *refs):
    count = len(distances)
    groups, outs = [refs[:count], refs[count : (1 + tiles) * count]], refs[(1 + tiles) * count :]
    mine, theirs = outs[:2]
    flip, zero = lax.axis_index("rows"), lax.axis_index("depth") == 0
    rhs = pair[...]
    for group in range(2):
        block = jnp.concatenate([chunk[...] for chunk in groups[group]], axis=0)
        outs[2 + 2 * group][...], outs[3 + 2 * group][...] = split(jnp.transpose(block))
        value = folded(*split(block), rhs)
        half_index = jnp.where(flip == 0, group, 1 - group)
        for i in range(count):
            first = value[(i * tiles) * share : (i * tiles + 1) * share]
            second = value[(i * tiles + 1) * share : (i * tiles + 2) * share]
            near = -jnp.where(zero, first, second)
            if group == 0:
                near = near + level[share_rows(distances[i], share), :]
            at = pl.ds(pl.multiple_of((i * 2 + half_index) * share, share), share)
            mine[at, :] = near
            theirs[at, :] = -jnp.where(zero, second, first)


def start_body(high, low, pair, out, lower):
    value = folded(high[...], low[...], pair[...])
    out[...] = value
    lower[...] = value[value.shape[0] // 2 :]


def base_body(high, low, part, far, out):
    half = far.shape[0]
    value = jnp.concatenate([part[:half, :], part[half:, :] + far[...]], axis=0)
    rows = jnp.concatenate(split(jnp.transpose(value)), axis=0)
    both = mm(rows, high[...]) + mm(rows, low[...])
    shots = both.shape[0] // 2
    out[...] = jnp.transpose(both[:shots] + both[shots:])


def near_body(inverse, three, corner, near_high, near_low, turned_high, turned_low):
    half = inverse.shape[1]
    quarter = half // 2
    three[0] = inverse[half : half + quarter, :quarter]
    three[1] = inverse[half + quarter :, :quarter]
    three[2] = inverse[half + quarter :, quarter:]
    corner[...] = inverse[half : half + quarter, quarter:]
    high, low = split(inverse[...])
    left_high, left_low = jnp.transpose(high), jnp.transpose(low)
    near = mm(left_high, high) + mm(left_high, low) + mm(left_low, high)
    near_high[...], near_low[...] = split(near)
    turned_high[...], turned_low[...] = left_high[:, half:], left_low[:, half:]


def far_body(turned_high, turned_low, three, corner, far_high, far_low):
    other = jnp.concatenate(
        [jnp.concatenate([three[0], corner[...]], axis=1), jnp.concatenate([three[1], three[2]], axis=1)], axis=0
    )
    high, low = split(other)
    far = mm(turned_high[...], high) + mm(turned_high[...], low) + mm(turned_low[...], high)
    far_high[...], far_low[...] = split(far)


def top_body(share, stages, near_high, near_low, far_high, far_low, *refs):
    batches = len(stages)
    sums, others, out, rest = refs[:batches], refs[batches : 2 * batches], refs[2 * batches], refs[2 * batches + 1]
    for number, distances in enumerate(stages):
        for i, distance in enumerate(distances):
            for group in range(2):
                rows = pl.ds((i * 2 + group) * share, share)
                rest[group, share_rows(distance, share), :] = sums[number][rows, :] + others[number][rows, :]
    flip = lax.axis_index("rows")
    out[...] = folded(near_high[...], near_low[...], beside(rest[flip])) + folded(
        far_high[...], far_low[...], beside(rest[1 - flip])
    )


def couple(tiles, share, stages, start, mine, peer, flats, both, store, pieces):
    depth = lax.axis_index("depth")
    both[depth] = mine[...]
    both[1 - depth] = peer[...]
    rows = [
        jnp.concatenate(
            [both[t, share_rows(distance, share), :] for distance in distances for t in range(tiles)], axis=0
        )
        for distances in stages
    ]
    size = start.shape[0] // pieces
    joined = all(flat.shape[1] % 128 == 0 for flat in flats)
    rights = [beside(jnp.concatenate(rows, axis=0))] if joined else [beside(row) for row in rows]
    for piece in range(pieces):
        at = slice(piece * size, (piece + 1) * size)
        highs, lows = [flat[at, :] for flat in flats[::2]], [flat[at, :] for flat in flats[1::2]]
        if joined:
            highs, lows = [jnp.concatenate(highs, axis=1)], [jnp.concatenate(lows, axis=1)]
        total = start[at, :]
        for high, low, right in zip(highs, lows, rights):
            total = total - folded(high, low, right)
        store(piece, at, total)


def couple_body(tiles, share, stages, start, mine, peer, *refs):
    *flats, out, answer, both, semaphore = refs
    copy = pltpu.make_async_copy(mine, answer.at[0, 1], semaphore)
    copy.start()

    def store(piece, at, total):
        out[at, :] = total

    couple(tiles, share, stages, start, mine, peer, flats, both, store, 1)
    copy.wait()


def final_body(tiles, share, stages, pieces, start, mine, peer, *refs):
    *flats, _, answer, both, held, semaphores = refs
    copies = []

    def store(piece, at, total):
        held[at, :] = total
        copies.append(pltpu.make_async_copy(held.at[at, :], answer.at[0, 0, at, :], semaphores.at[piece]))
        copies[-1].start()

    couple(tiles, share, stages, start, mine, peer, flats, both, store, pieces)
    for copy in copies:
        copy.wait()


def snake(count):
    return list(range(0, count, 2)) + list(range(1, count, 2))[::-1]


def per_device(sources, factor, block_mask, inverse_diagonal):
    shots_count = lax.axis_size("shots")
    rows_count = lax.axis_size("rows")
    depth_count = lax.axis_size("depth")
    assert rows_count == 2 and depth_count == 2 and sources.shape[1] == 2 and shots_count % 2 == 0
    order = snake(shots_count)
    ahead = [(order[i], order[(i + 1) % shots_count]) for i in range(shots_count)]
    behind = [(b, a) for a, b in ahead]
    swap = [(0, 1), (1, 0)]

    tiles, share, width = factor.shape[1:]
    half = width // rows_count
    block = width // block_mask.shape[3]
    shots = sources.shape[3]
    quarter = half // 2

    hold = pltpu.with_memory_space_constraint(factor, pltpu.HBM)
    *lefts, right = call(
        halves_body,
        [((share, half), F32)] * tiles + [((tiles, share, half), F32)],
        [hold],
        0,
        scratch=[pltpu.SemaphoreType.DMA((tiles + 1,))],
        plain=(0,),
    )
    far_right = lax.ppermute(right, "rows", swap)
    far_lefts = [lax.ppermute(left, "rows", [(1, 0)]) for left in lefts]
    heavy = 8 * share * width * half
    own, high0, low0, pair0 = call(
        functools.partial(first_body, tiles, share, block),
        [((tiles * share, half), F32)] + [((width, half), BF16)] * 2 + [((half, 2 * shots), BF16)],
        [part_of(block_mask, 0), part_of(factor, 0), part_of(inverse_diagonal, 0, 0), part_of(sources, 0, 0)],
        heavy * tiles,
    )
    chains = [own]
    for tile in range(tiles):
        chains += call(
            functools.partial(second_body, tile, share, block),
            [((share, half), F32)],
            [part_of(block_mask, 0), far_lefts[tile], far_right, high0, low0],
            heavy,
        )

    hops = shots_count // 2
    stages, pieces = [[0]], [[[piece] for piece in chains]]
    forward, backward = list(chains), list(chains)
    for hop in range(1, hops):
        for number in range(len(chains)):
            forward[number] = lax.ppermute(forward[number], "shots", ahead)
            backward[number] = lax.ppermute(backward[number], "shots", behind)
        if hop == 1:
            stages[0] += [-1, 1]
            for number in range(len(chains)):
                pieces[0][number] += [forward[number], backward[number]]
        else:
            stages.append([-hop, hop])
            pieces.append([list(pair) for pair in zip(forward, backward)])
    stages.append([hops])
    pieces.append(
        [[lax.ppermute(forward[0], "shots", ahead)]]
        + [[lax.ppermute(backward[number], "shots", behind)] for number in range(1, len(chains))]
    )

    part0, lower0 = call(
        start_body, [((width, shots), F32), ((half, shots), F32)], [high0, low0, pair0], 8 * width * half * shots
    )
    far0 = lax.ppermute(lower0, "rows", swap)
    (base0,) = call(base_body, [((half, shots), F32)], [high0, low0, part0, far0], 8 * width * half * shots)

    three1, corner1, *squares = call(
        near_body,
        [((3, quarter, quarter), F32), ((quarter, quarter), F32)] + [((half, half), BF16)] * 4,
        [part_of(inverse_diagonal, 0, 1)],
        6 * half * half * width,
    )
    squares[2:] = call(
        far_body,
        [((half, half), BF16)] * 2,
        [*squares[2:], lax.ppermute(three1, "rows", swap), lax.ppermute(corner1, "rows", [(0, 1)])],
        6 * half * half * half,
    )

    sums, others, flats = [], [], [[], []]
    for distances, piece in zip(stages, pieces):
        count = len(distances)
        deep = count * tiles * share
        mine, theirs, *flat = call(
            functools.partial(hop_body, tiles, share, distances),
            [((2 * count * share, shots), F32)] * 2 + [((half, deep), BF16)] * 4,
            [pair0, part_of(sources, 0, 1)]
            + piece[0]
            + [chunk for row in zip(*piece[1:]) for chunk in row],
            16 * deep * half * shots,
        )
        total = mine + lax.ppermute(theirs, "depth", swap)
        sums.append(total)
        others.append(lax.ppermute(total, "rows", swap))
        flats[0] += flat[:2]
        flats[1] += flat[2:]

    (top,) = call(
        functools.partial(top_body, share, stages),
        [((half, shots), F32)],
        [*squares, *sums, *others],
        16 * half * half * shots,
        scratch=[pltpu.VMEM((2, half, shots), F32)],
    )
    far_top = lax.ppermute(top, "rows", swap)
    peer_top = lax.ppermute(top, "depth", swap)
    peer_far = lax.ppermute(far_top, "depth", swap)
    work = 8 * half * width * shots
    shape = ((1, 2, half, shots), F32)
    almost, answer = call(
        functools.partial(couple_body, tiles, share, stages),
        [((half, shots), F32), shape],
        [base0, top, peer_top, *flats[0]],
        work,
        scratch=[pltpu.VMEM((2, half, shots), F32), pltpu.SemaphoreType.DMA],
        placed=(1,),
    )
    pieces = 4 if half % 512 == 0 else 1
    ins = [almost, far_top, peer_far, *flats[1], answer]
    (answer,) = call(
        functools.partial(final_body, tiles, share, stages, pieces),
        [shape],
        ins,
        work,
        scratch=[
            pltpu.VMEM((2, half, shots), F32),
            pltpu.VMEM((half, shots), F32),
            pltpu.SemaphoreType.DMA((pieces,)),
        ],
        plain=(len(ins) - 1,),
        placed=(0,),
        alias={len(ins) - 1: 0},
    )
    return answer


def solution(mesh):
    placed = (
        P("depth", None, "rows", "shots"),
        P("depth", None, ("rows", "shots"), None),
        P("depth", None, None, None),
        P("depth", None, None, "rows"),
    )

    return jax.shard_map(
        per_device,
        mesh=mesh,
        in_specs=placed,
        out_specs=P("depth", None, "rows", "shots"),
        check_vma=False,
    )
```

```python
import functools

import jax
import jax.numpy as jnp
from jax import lax
from jax.experimental import pallas as pl
from jax.experimental.pallas import tpu as pltpu
from jax.sharding import PartitionSpec as P


F32, BF16 = jnp.float32, jnp.bfloat16
VMEM = pl.BlockSpec(memory_space=pltpu.VMEM)
HBM = pl.BlockSpec(memory_space=pltpu.HBM)
GRANT = 12 * 1024 * 1024


def split(value):
    high = value.astype(BF16)
    return high, (value - high.astype(F32)).astype(BF16)


def beside(value):
    return jnp.concatenate(split(value), axis=1)


def mm(left, right, contract=((1,), (0,))):
    return lax.dot_general(left, right, (contract, ((), ())), preferred_element_type=F32)


def folded(left_high, left_low, right_pair, contract=((1,), (0,))):
    both = mm(left_high, right_pair, contract) + mm(left_low, right_pair, contract)
    width = both.shape[1] // 2
    return both[:, :width] + both[:, width:]


def part_of(array, *index):
    return array, index


def call(body, outs, ins, flops, scratch=(), plain=(), placed=(), alias=None):
    arrays = [pltpu.with_memory_space_constraint(x[0], pltpu.HBM) if isinstance(x, tuple) else x for x in ins]
    parts = [x[1] if isinstance(x, tuple) else None for x in ins]
    picked = [i for i, index in enumerate(parts) if index is not None]

    def space(array):
        return pltpu.SMEM if array.dtype == jnp.int32 else pltpu.VMEM

    def run(*refs):
        refs = list(refs)
        if picked:
            semaphores = refs.pop()
            buffers = [refs.pop() for _ in picked][::-1]
            copies = []
            for number, i in enumerate(picked):
                source = refs[i].at[parts[i]]
                copies.append(pltpu.make_async_copy(source, buffers[number], semaphores.at[number]))
                copies[-1].start()
                refs[i] = buffers[number]
            for copy in copies:
                copy.wait()
        body(*refs)

    held = [space(arrays[i])(arrays[i].shape[len(parts[i]) :], arrays[i].dtype) for i in picked]
    if picked:
        held.append(pltpu.SemaphoreType.DMA((len(picked),)))
    moved = sum(x.size * x.dtype.itemsize for x in arrays)
    return pl.pallas_call(
        run,
        out_shape=[jax.ShapeDtypeStruct(shape, kind) for shape, kind in outs],
        in_specs=[HBM if index is not None or i in plain else VMEM for i, index in enumerate(parts)],
        out_specs=[HBM if i in placed else VMEM for i in range(len(outs))],
        scratch_shapes=list(scratch) + held,
        input_output_aliases=alias or {},
        compiler_params=pltpu.CompilerParams(vmem_limit_bytes=GRANT),
        cost_estimate=pl.CostEstimate(flops=flops, bytes_accessed=moved, transcendentals=0),
    )(*arrays)


def spot(distance):
    count, index = lax.axis_size("shots"), lax.axis_index("shots")
    at = lax.rem(jnp.where(index % 2 == 0, index // 2, count - 1 - index // 2) + (distance + count), count)
    return jnp.where(2 * at < count, 2 * at, 2 * (count - 1 - at) + 1)


def share_rows(distance, share):
    return pl.ds(pl.multiple_of(spot(distance) * share, share), share)


def product(tiles, share, block, group, mask, factor, high, low, out):
    width = high.shape[0]
    first = ((group * lax.axis_size("shots") + lax.axis_index("shots")) * share) // block
    size = min(share, block)
    parts = []
    for tile in tiles:
        for band in range(share // size):
            pieces = []
            for column in range(width // block):
                keep = mask[tile, first + band, column].astype(F32)
                pieces.append(factor(tile, slice(band * size, (band + 1) * size), column * block, block) * keep)
            parts.append(jnp.concatenate(pieces, axis=1))
    stacked = jnp.concatenate(split(jnp.concatenate(parts, axis=0)), axis=0)
    both = mm(stacked, high[...]) + mm(stacked, low[...])
    out[...] = both[: len(tiles) * share] + both[len(tiles) * share :]


def first_body(tiles, share, block, mask, factor, inverse, own, out, high, low, pair):
    high[...], low[...] = split(inverse[...])
    pair[...] = beside(own[...])

    def load(tile, rows, start, size):
        return factor[tile, rows, start : start + size]

    product(range(tiles), share, block, lax.axis_index("rows"), mask, load, high, low, out)


def second_body(tiles, share, block, mask, received, high, low, out):
    half = high.shape[1]
    flip = lax.axis_index("rows")

    def load(tile, rows, start, size):
        if start >= half:
            return received[tile, rows, start - half : start - half + size]
        left = received[tile, share + rows.start : share + rows.stop, start : start + size]
        return jnp.where(flip == 0, left, 0.0)

    product(range(tiles), share, block, 1 - flip, mask, load, high, low, out)


def halves_body(factor, inverse, out, semaphores):
    tiles, share, width = factor.shape[1:]
    half = width // 2
    quarter, slab = half // 2, half // 8
    flip = lax.axis_index("rows")

    def copy(source, target, number):
        return pltpu.make_async_copy(source, target, semaphores.at[number])

    rights = [copy(factor.at[0, t, :, half:], out.at[t, :share, :], t) for t in range(tiles)]
    for each in rights:
        each.start()

    @pl.when(flip == 1)
    def _():
        lefts = [copy(factor.at[0, t, :, :half], out.at[t, share : 2 * share, :], tiles + t) for t in range(tiles)]
        for each in lefts:
            each.start()
        for each in lefts:
            each.wait()

    @pl.when(flip == 0)
    def _():
        corners = []
        for t in range(tiles):
            for side in range(2):
                top = half + (2 * t + side) * slab
                corners.append(
                    copy(
                        inverse.at[0, 1, top : top + slab, quarter:half],
                        out.at[t, share : share + slab, side * quarter : (side + 1) * quarter],
                        tiles + 2 * t + side,
                    )
                )
        for each in corners:
            each.start()
        for each in corners:
            each.wait()

    for each in rights:
        each.wait()


def hop_body(tiles, share, distances, pair, level, *refs):
    count, chunks = len(distances), (len(refs) - 6) // 2
    groups, outs = [refs[:chunks], refs[chunks : 2 * chunks]], refs[2 * chunks :]
    mine, theirs = outs[:2]
    flip, zero = lax.axis_index("rows"), lax.axis_index("depth") == 0
    rhs = pair[...]
    for group in range(2):
        block = jnp.concatenate([chunk[...] for chunk in groups[group]], axis=0)
        outs[2 + 2 * group][...], outs[3 + 2 * group][...] = split(jnp.transpose(block))
        value = folded(*split(block), rhs)
        half_index = jnp.where(flip == 0, group, 1 - group)
        for i in range(count):
            first = value[(i * tiles) * share : (i * tiles + 1) * share]
            second = value[(i * tiles + 1) * share : (i * tiles + 2) * share]
            near = -jnp.where(zero, first, second)
            if group == 0:
                near = near + level[share_rows(distances[i], share), :]
            at = pl.ds(pl.multiple_of((i * 2 + half_index) * share, share), share)
            mine[at, :] = near
            theirs[at, :] = -jnp.where(zero, second, first)


def start_body(high, low, pair, inverse, sources, out, bulk, level, semaphores):
    half = level.shape[0]
    quarter, slab, shots = half // 2, half // 4, level.shape[1]

    def copy(row, size, column, target, number):
        source = inverse.at[0, 1, half + row : half + row + size, column : column + quarter]
        return pltpu.make_async_copy(source, target, semaphores.at[number])

    copies = [
        copy(0, quarter, 0, bulk.at[:quarter, :quarter], 0),
        copy(quarter, quarter, quarter, bulk.at[:quarter, quarter:], 1),
        copy(quarter, slab, 0, bulk.at[quarter : quarter + slab, :quarter], 2),
        copy(quarter + slab, slab, 0, bulk.at[quarter : quarter + slab, quarter:], 3),
        pltpu.make_async_copy(sources.at[0, 1], level, semaphores.at[4]),
    ]
    for each in copies:
        each.start()
    value = folded(high[...], low[...], pair[...])
    out[...] = value
    for number in range(half // shots):
        first = half + number * shots
        bulk[quarter + slab :, number * shots : (number + 1) * shots] = value[first : first + shots]
    for each in copies:
        each.wait()


def base_body(high, low, part, bulk, out):
    half, shots = out.shape
    far = jnp.concatenate(
        [bulk[bulk.shape[0] - shots :, number * shots : (number + 1) * shots] for number in range(half // shots)], axis=0
    )
    value = jnp.concatenate([part[:half, :], part[half:, :] + far], axis=0)
    stacked = jnp.concatenate(split(jnp.transpose(value)), axis=0)
    both = mm(stacked, high[...]) + mm(stacked, low[...])
    out[...] = jnp.transpose(both[:shots] + both[shots:])


def near_body(inverse, near_high, near_low, turned_high, turned_low):
    half = inverse.shape[1]
    high, low = split(inverse[...])
    left_high, left_low = jnp.transpose(high), jnp.transpose(low)
    near = mm(left_high, high) + mm(left_high, low) + mm(left_low, high)
    near_high[...], near_low[...] = split(near)
    turned_high[...], turned_low[...] = left_high[:, half:], left_low[:, half:]


def far_body(share, turned_high, turned_low, bulk, received, far_high, far_low):
    half = bulk.shape[1]
    quarter, slab = half // 2, half // 4
    piece = slab // received.shape[0]
    corner = jnp.concatenate(
        [
            received[t, share : share + piece, side * quarter : (side + 1) * quarter]
            for t in range(received.shape[0])
            for side in range(2)
        ],
        axis=0,
    )
    corner = jnp.where(lax.axis_index("rows") == 1, corner, 0.0)
    bottom = jnp.concatenate([bulk[quarter : quarter + slab, :quarter], bulk[quarter : quarter + slab, quarter:]], axis=0)
    other = jnp.concatenate(
        [
            jnp.concatenate([bulk[:quarter, :quarter], corner], axis=1),
            jnp.concatenate([bottom, bulk[:quarter, quarter:]], axis=1),
        ],
        axis=0,
    )
    high, low = split(other)
    far = mm(turned_high[...], high) + mm(turned_high[...], low) + mm(turned_low[...], high)
    far_high[...], far_low[...] = split(far)


def top_body(share, stages, near_high, near_low, far_high, far_low, *refs):
    batches = len(stages)
    sums, others, out, rest = refs[:batches], refs[batches : 2 * batches], refs[2 * batches], refs[2 * batches + 1]
    for number, distances in enumerate(stages):
        for i, distance in enumerate(distances):
            for group in range(2):
                rows = pl.ds((i * 2 + group) * share, share)
                rest[group, share_rows(distance, share), :] = sums[number][rows, :] + others[number][rows, :]
    flip = lax.axis_index("rows")
    out[...] = folded(near_high[...], near_low[...], beside(rest[flip])) + folded(
        far_high[...], far_low[...], beside(rest[1 - flip])
    )


def couple(tiles, share, stages, start, mine, peer, flats, both, store, pieces):
    depth = lax.axis_index("depth")
    both[depth] = mine[...]
    both[1 - depth] = peer[...]
    rows = [
        jnp.concatenate(
            [both[t, share_rows(distance, share), :] for distance in distances for t in range(tiles)], axis=0
        )
        for distances in stages
    ]
    size = start.shape[0] // pieces
    joined = all(flat.shape[1] % 128 == 0 for flat in flats)
    rights = [beside(jnp.concatenate(rows, axis=0))] if joined else [beside(row) for row in rows]
    for piece in range(pieces):
        at = slice(piece * size, (piece + 1) * size)
        highs, lows = [flat[at, :] for flat in flats[::2]], [flat[at, :] for flat in flats[1::2]]
        if joined:
            highs, lows = [jnp.concatenate(highs, axis=1)], [jnp.concatenate(lows, axis=1)]
        total = start[at, :]
        for high, low, right in zip(highs, lows, rights):
            total = total - folded(high, low, right)
        store(piece, at, total)


def couple_body(tiles, share, stages, start, mine, peer, *refs):
    *flats, out, answer, both, semaphore = refs
    copy = pltpu.make_async_copy(mine, answer.at[0, 1], semaphore)
    copy.start()

    def store(piece, at, total):
        out[at, :] = total

    couple(tiles, share, stages, start, mine, peer, flats, both, store, 1)
    copy.wait()


def final_body(tiles, share, stages, pieces, start, mine, peer, *refs):
    *flats, _, answer, both, held, semaphores = refs
    copies = []

    def store(piece, at, total):
        held[at, :] = total
        copies.append(pltpu.make_async_copy(held.at[at, :], answer.at[0, 0, at, :], semaphores.at[piece]))
        copies[-1].start()

    couple(tiles, share, stages, start, mine, peer, flats, both, store, pieces)
    for copy in copies:
        copy.wait()


def snake(count):
    return list(range(0, count, 2)) + list(range(1, count, 2))[::-1]


def per_device(sources, factor, block_mask, inverse_diagonal):
    shots_count = lax.axis_size("shots")
    rows_count = lax.axis_size("rows")
    depth_count = lax.axis_size("depth")
    assert rows_count == 2 and depth_count == 2 and sources.shape[1] == 2
    assert shots_count % 2 == 0 and shots_count >= 4
    order = snake(shots_count)
    ahead = [(order[i], order[(i + 1) % shots_count]) for i in range(shots_count)]
    behind = [(b, a) for a, b in ahead]
    swap = [(0, 1), (1, 0)]

    tiles, share, width = factor.shape[1:]
    half = width // rows_count
    block = width // block_mask.shape[3]
    shots = sources.shape[3]
    quarter = half // 2

    assert tiles == 2 and half % shots == 0
    hold_factor, hold_inverse, hold_sources = (
        pltpu.with_memory_space_constraint(x, pltpu.HBM) for x in (factor, inverse_diagonal, sources)
    )
    (halves,) = call(
        halves_body,
        [((tiles, share + max(share, half // 8), half), F32)],
        [hold_factor, hold_inverse],
        0,
        scratch=[pltpu.SemaphoreType.DMA((3 * tiles,))],
        plain=(0, 1),
    )
    received = lax.ppermute(halves, "rows", swap)
    heavy = 8 * tiles * share * width * half
    own, high0, low0, pair0 = call(
        functools.partial(first_body, tiles, share, block),
        [((tiles * share, half), F32)] + [((width, half), BF16)] * 2 + [((half, 2 * shots), BF16)],
        [part_of(block_mask, 0), part_of(factor, 0), part_of(inverse_diagonal, 0, 0), part_of(sources, 0, 0)],
        heavy,
    )
    (far,) = call(
        functools.partial(second_body, tiles, share, block),
        [((tiles * share, half), F32)],
        [part_of(block_mask, 0), received, high0, low0],
        heavy,
    )

    hops = shots_count // 2
    stages, pieces = [[0]], [[[own], [far]]]
    forward, backward = [own, far], [own, far]
    for hop in range(1, hops):
        for number in range(2):
            forward[number] = lax.ppermute(forward[number], "shots", ahead)
            backward[number] = lax.ppermute(backward[number], "shots", behind)
        if hop + 1 < hops:
            stages[0] += [-hop, hop]
            for number in range(2):
                pieces[0][number] += [forward[number], backward[number]]
        else:
            stages.append([-hop, hop])
            pieces.append([list(pair) for pair in zip(forward, backward)])
    stages.append([hops])
    pieces.append(
        [
            [
                lax.ppermute(forward[number][:share], "shots", ahead),
                lax.ppermute(backward[number][share:], "shots", behind),
            ]
            for number in range(2)
        ]
    )

    part0, bulk, level1 = call(
        start_body,
        [((width, shots), F32), ((quarter + half // 4 + shots, half), F32), ((half, shots), F32)],
        [high0, low0, pair0, hold_inverse, hold_sources],
        8 * width * half * shots,
        scratch=[pltpu.SemaphoreType.DMA((5,))],
        plain=(3, 4),
    )
    far_bulk = lax.ppermute(bulk, "rows", swap)
    (base0,) = call(base_body, [((half, shots), F32)], [high0, low0, part0, far_bulk], 8 * width * half * shots)

    near_high, near_low, *turned = call(
        near_body, [((half, half), BF16)] * 4, [part_of(inverse_diagonal, 0, 1)], 6 * half * half * width
    )
    squares = [near_high, near_low]
    squares += call(
        functools.partial(far_body, share),
        [((half, half), BF16)] * 2,
        [*turned, far_bulk, received],
        6 * half * half * half,
    )

    sums, others, flats = [], [], [[], []]
    for distances, piece in zip(stages, pieces):
        count = len(distances)
        deep = count * tiles * share
        mine, theirs, *flat = call(
            functools.partial(hop_body, tiles, share, distances),
            [((2 * count * share, shots), F32)] * 2 + [((half, deep), BF16)] * 4,
            [pair0, level1] + piece[0] + piece[1],
            16 * deep * half * shots,
        )
        total = mine + lax.ppermute(theirs, "depth", swap)
        sums.append(total)
        others.append(lax.ppermute(total, "rows", swap))
        flats[0] += flat[:2]
        flats[1] += flat[2:]

    (top,) = call(
        functools.partial(top_body, share, stages),
        [((half, shots), F32)],
        [*squares, *sums, *others],
        16 * half * half * shots,
        scratch=[pltpu.VMEM((2, half, shots), F32)],
    )
    far_top = lax.ppermute(top, "rows", swap)
    peer_top = lax.ppermute(top, "depth", swap)
    peer_far = lax.ppermute(far_top, "depth", swap)
    work = 8 * half * width * shots
    shape = ((1, 2, half, shots), F32)
    almost, answer = call(
        functools.partial(couple_body, tiles, share, stages),
        [((half, shots), F32), shape],
        [base0, top, peer_top, *flats[0]],
        work,
        scratch=[pltpu.VMEM((2, half, shots), F32), pltpu.SemaphoreType.DMA],
        placed=(1,),
    )
    pieces = 4 if half % 512 == 0 else 1
    ins = [almost, far_top, peer_far, *flats[1], answer]
    (answer,) = call(
        functools.partial(final_body, tiles, share, stages, pieces),
        [shape],
        ins,
        work,
        scratch=[
            pltpu.VMEM((2, half, shots), F32),
            pltpu.VMEM((half, shots), F32),
            pltpu.SemaphoreType.DMA((pieces,)),
        ],
        plain=(len(ins) - 1,),
        placed=(0,),
        alias={len(ins) - 1: 0},
    )
    return answer


def solution(mesh):
    placed = (
        P("depth", None, "rows", "shots"),
        P("depth", None, ("rows", "shots"), None),
        P("depth", None, None, None),
        P("depth", None, None, "rows"),
    )

    return jax.shard_map(
        per_device,
        mesh=mesh,
        in_specs=placed,
        out_specs=P("depth", None, "rows", "shots"),
        check_vma=False,
    )
```
